32 devices in a mesh: scene: 2 (over y), seq: 4 (over z), head: 2 (over x), band: 2 (over core).
Axes of the slice: x: 2, y: 2, z: 4, core: 2. Of those that a mesh axis runs over, the one named last changes fastest.
Arguments:
- tokens: bfloat16 [8, 12, 37, 1024], P(('scene', 'seq'), ('head', 'band')), parts along dimension 0, may hold values from -6 to 6
- frame_gain: float32 [1024], replicated, may hold values from 0.5 to 1.5
- frame_qkv: bfloat16 [3, 1024, 1024], P(None, None, 'head'), may hold values from -6 to 6
- frame_out: bfloat16 [1024, 1024], P('head'), may hold values from -0.1875 to 0.1875
- global_gain: float32 [1024], replicated, may hold values from 0.5 to 1.5
- global_qkv: bfloat16 [3, 1024, 1024], P(None, None, 'head'), may hold values from -6 to 6
- global_out: bfloat16 [1024, 1024], P('head'), may hold values from -0.1875 to 0.1875
- head_gain: float32 [2048], replicated, may hold values from 0.5 to 1.5
- head_proj: bfloat16 [2048, 256], replicated, may hold values from -0.125 to 0.125
- head_bias: float32 [256], replicated, may hold values from -3 to 3
- head_conv: bfloat16 [3, 3, 256, 256], replicated, may hold values from -0.125 to 0.125
Outputs:
- blocks: bfloat16 [8, 12, 37, 1024], P(('scene', 'seq'), ('head', 'band')), parts along dimension 0
- features: bfloat16 [8, 12, 37, 256], P(('scene', 'seq'), ('head', 'band')), parts along dimension 0
The draws below stay inside these ranges and needn't reach their ends.
There are 2 independent parts, one for each index of `scene`. The reference program is written for one: setup_inputs(seed, part) draws one part's arguments, and reference() takes and returns one part's arrays. A program takes and returns all parts, laid end to end along the dimension named above; an argument that names none is the same for every part. Nothing has to cross between parts.
All inputs are finite; a program needn't handle non-finite values.
Results may differ from the reference program's by a relative error of at most 0.017.
Values may be sent and summed in bfloat16 or wider, within the bound.
No kernel may reach another device: no remote copies, remote signals or barrier semaphores. Data moves between devices by JAX's collectives and lax.ppermute only.
A program may use at most 256 MiB of HBM per device.

```python
import math
import jax
import jax.numpy as jnp
from jax import lax

D = 1024
HEADS = 16
HD = 64
CH = 256
PC = 37
PR = 12
FRAMES = 4


def projection_draw(key):
    first_key, second_key = jax.random.split(key, 2)
    base = jax.random.truncated_normal(first_key, -6.0, 6.0, (3, D, D), jnp.float32) * D ** (-0.5)
    head_scale = jnp.exp(jax.random.uniform(second_key, (2, HEADS), jnp.float32, math.log(1.3), math.log(2.2)))
    columns = jnp.repeat(head_scale, HD, axis=1)
    queries = base[0] * columns[0]
    keys_part = base[1] * columns[1]
    stacked = jnp.stack([queries, keys_part, base[2]])
    return jnp.clip(stacked, -6.0, 6.0).astype(jnp.bfloat16)


def draw_frame_qkv(key, part):
    return projection_draw(jax.random.fold_in(key, 11))


def draw_global_qkv(key, part):
    return projection_draw(jax.random.fold_in(key, 23))


def level_of(key, shape, cuts, low, largest):
    level, own = 1.0, jax.random.fold_in(key, 6)
    for axis_at, blocks in cuts:
        heights = jnp.exp(jax.random.uniform(jax.random.fold_in(own, axis_at), (blocks,), jnp.float32, low / len(cuts), largest / len(cuts)))
        level = level * jnp.repeat(heights, shape[axis_at] // blocks).reshape([-1 if axis == axis_at else 1 for axis in range(len(shape))])
    return level


def noise(own_key, shape, scale, most, shards=(), held_as=jnp.bfloat16):
    values = jax.random.normal(own_key, shape, jnp.float32) * scale
    if len(shards) > 0:
        values = level_of(own_key, shape, shards, -0.22, 0.18) * values
    return jnp.clip(values, min=-most, max=most).astype(held_as)


def setup_inputs(seed: int = 0, part: int = 0) -> dict:
    key_of = jax.random.split(jax.random.key(seed), 12)
    own_keys = jax.random.split(jax.random.fold_in(key_of[11], part), 12)
    tokens = noise(own_keys[0], (FRAMES, PR, PC, D), 1.0, 6.0, ((0, 4), (1, 4)))
    frame_gain = jnp.clip(1.0 + 0.1 * jax.random.normal(key_of[1], (D,), jnp.float32), 0.5, 1.5)
    frame_qkv = draw_frame_qkv(jax.random.fold_in(key_of[11], 71), part)
    frame_out = noise(key_of[3], (D, D), D ** -0.5, 0.1875, ((0, 2),))
    global_gain = jnp.clip(1.0 + 0.1 * jax.random.normal(key_of[4], (D,), jnp.float32), 0.5, 1.5)
    global_qkv = draw_global_qkv(jax.random.fold_in(key_of[11], 71), part)
    global_out = noise(key_of[6], (D, D), D ** -0.5, 0.1875, ((0, 2),))
    head_gain = jnp.clip(1.0 + 0.1 * jax.random.normal(key_of[7], (2 * D,), jnp.float32), 0.5, 1.5)
    head_proj = noise(key_of[8], (2 * D, CH), (2 * D) ** -0.5, 0.125)
    head_bias = noise(key_of[9], (CH,), 0.5, 3.0, (), jnp.float32)
    head_conv = noise(key_of[10], (3, 3, CH, CH), (9 * CH) ** -0.5, 0.125)
    return {"tokens": tokens, "frame_gain": frame_gain, "frame_qkv": frame_qkv, "frame_out": frame_out, "global_gain": global_gain, "global_qkv": global_qkv, "global_out": global_out, "head_gain": head_gain, "head_proj": head_proj, "head_bias": head_bias, "head_conv": head_conv}


norm_eps = 1e-06
head_eps = 1e-05

def layer_norm(values, gain, epsilon):
    centre = values - lax.optimization_barrier(jnp.mean(values, axis=-1, keepdims=True))
    spread = lax.optimization_barrier(jnp.mean(centre * centre, axis=-1, keepdims=True))
    return centre * lax.rsqrt(spread + epsilon) * gain

def attend_head(triple):
    queries, keys_all, values_all = triple
    scores = jnp.dot(queries, keys_all.T, preferred_element_type=jnp.float32) * HD ** (-0.5)
    probs = jnp.exp(scores - lax.optimization_barrier(jnp.max(scores, axis=-1, keepdims=True)))
    mixed = jnp.dot(probs.astype(jnp.bfloat16), values_all, preferred_element_type=jnp.float32)
    return mixed / lax.optimization_barrier(jnp.sum(probs, axis=-1, keepdims=True))

def by_heads(matrix):
    return matrix.reshape(matrix.shape[0], HEADS, HD).transpose(1, 0, 2)

def attention(queries, keys_all, values_all):
    mixed = lax.map(attend_head, (by_heads(queries), by_heads(keys_all), by_heads(values_all)))
    return mixed.transpose(1, 0, 2).reshape(queries.shape[0], D).astype(jnp.bfloat16)

def attention_block(inputs, gain, qkv_weight, out_weight, wide):
    frames_now, per_frame = (inputs.shape[0], inputs.shape[1])
    normed = layer_norm(inputs.astype(jnp.float32), gain, norm_eps).astype(jnp.bfloat16)
    flattened = normed.reshape(frames_now * per_frame, D)
    query_rows = jnp.dot(flattened, qkv_weight[0], preferred_element_type=jnp.float32).astype(jnp.bfloat16)
    key_rows = jnp.dot(flattened, qkv_weight[1], preferred_element_type=jnp.float32).astype(jnp.bfloat16)
    value_rows = jnp.dot(flattened, qkv_weight[2], preferred_element_type=jnp.float32).astype(jnp.bfloat16)
    query_frames = query_rows.reshape(frames_now, per_frame, D)
    if wide:

        def one_frame(frame_queries):
            return attention(frame_queries, key_rows, value_rows)
        mixed = lax.map(one_frame, query_frames)
    else:

        def own_frame(triple):
            return attention(triple[0], triple[1], triple[2])
        mixed = lax.map(own_frame, (query_frames, key_rows.reshape(frames_now, per_frame, D), value_rows.reshape(frames_now, per_frame, D)))
    branch = jnp.dot(mixed.reshape(-1, D), out_weight, preferred_element_type=jnp.float32)
    merged = inputs.astype(jnp.float32).reshape(-1, D) + branch
    return merged.astype(jnp.bfloat16).reshape(inputs.shape)

def reference(tokens, frame_gain, frame_qkv, frame_out, global_gain, global_qkv, global_out, head_gain, head_proj, head_bias, head_conv):
    inputs = tokens.reshape(FRAMES, PR * PC, D)
    first = attention_block(inputs, frame_gain, frame_qkv, frame_out, False)
    second = attention_block(first, global_gain, global_qkv, global_out, True)
    stacked = jnp.concatenate([first.astype(jnp.float32), second.astype(jnp.float32)], axis=-1)
    normed = layer_norm(stacked, head_gain, head_eps).astype(jnp.bfloat16)
    projected = jnp.dot(normed.reshape(-1, 2 * D), head_proj, preferred_element_type=jnp.float32) + head_bias
    projected = projected.astype(jnp.bfloat16).reshape(FRAMES, PR, PC, CH)
    padded = jnp.pad(projected, ((0, 0), (1, 1), (1, 1), (0, 0)))
    totals = jnp.zeros((FRAMES, PR, PC, CH), jnp.float32)
    for offset_row in range(3):
        for offset_col in range(3):
            window = padded[:, offset_row:offset_row + PR, offset_col:offset_col + PC].astype(jnp.float32)
            totals = totals + jnp.einsum('frcx,xy->frcy', window, head_conv[offset_row, offset_col].astype(jnp.float32))
    return (second.reshape(FRAMES, PR, PC, D), totals.astype(jnp.bfloat16))
```

```python
import functools

import jax
import jax.numpy as jnp
from jax import lax
from jax.experimental import pallas as pl
from jax.experimental.pallas import tpu as pltpu
from jax.sharding import PartitionSpec as P

HD = 64
LANES = 128
LOG2E = 1.4426950408889634

norm_eps = 1e-06
head_eps = 1e-05

VM = pl.BlockSpec(memory_space=pltpu.VMEM)
SM = pl.BlockSpec(memory_space=pltpu.SMEM)
F32 = jnp.float32
BF16 = jnp.bfloat16


def swap(value, axis, distance):
    size = lax.axis_size(axis)
    return lax.ppermute(value, axis, [(i, i ^ distance) for i in range(size)])


def swap_both(value, axes, distances):
    (outer, inner), (a, b) = axes, distances
    if a == 0 or b == 0:
        return swap(value, inner if a == 0 else outer, a + b)
    rows, cols = lax.axis_size(outer), lax.axis_size(inner)
    pairs = [
        (i * cols + j, (i ^ a) * cols + (j ^ b)) for i in range(rows) for j in range(cols)
    ]
    return lax.ppermute(value, axes, pairs)


def call(kernel, outs, args, flops=0, exps=0, scratch=(), limit=32 << 20):
    moved = sum(a.size * a.dtype.itemsize for a in args)
    moved += sum(o.size * o.dtype.itemsize for o in outs)
    return pl.pallas_call(
        kernel,
        out_shape=outs,
        in_specs=[SM if a.dtype == jnp.int32 else VM for a in args],
        out_specs=[VM] * len(outs),
        scratch_shapes=list(scratch),
        compiler_params=pltpu.CompilerParams(vmem_limit_bytes=limit),
        cost_estimate=pl.CostEstimate(
            flops=int(flops), transcendentals=int(exps), bytes_accessed=int(moved)
        ),
    )(*args)


def shape(dims, dtype=BF16):
    return jax.ShapeDtypeStruct(tuple(dims), dtype)


def dot(a, b):
    return jnp.dot(a, b, preferred_element_type=F32)


def normalise(values, gain, epsilon):
    centre = values - jnp.mean(values, axis=-1, keepdims=True)
    spread = jnp.mean(centre * centre, axis=-1, keepdims=True)
    return centre * lax.rsqrt(spread + epsilon) * gain


def gather_rows(rows_ref, base, pad, grid_ref):
    frames, height, width, _ = grid_ref.shape
    at = base
    for f in range(frames):
        for r in range(height):
            rows_ref[at : at + width, :] = grid_ref[f, r].astype(F32)
            at += width
    last = grid_ref[frames - 1, height - 1, width - 1 : width, :].astype(F32)
    for extra in range(at, base + pad):
        rows_ref[extra : extra + 1, :] = last


def scatter_rows(grid_ref, rows_ref):
    frames, height, width, _ = grid_ref.shape
    at = 0
    for f in range(frames):
        for r in range(height):
            grid_ref[f, r] = rows_ref[at : at + width, :].astype(grid_ref.dtype)
            at += width


def qkv_kernel(x_ref, gain_ref, w_ref, q_ref, kv_ref, rows_ref):
    cols = q_ref.shape[1]
    gather_rows(rows_ref, 0, rows_ref.shape[0], x_ref)
    normed = normalise(rows_ref[...], gain_ref[...], norm_eps).astype(BF16)
    kv_ref[:, :cols] = dot(normed, w_ref[1]).astype(BF16)
    kv_ref[:, cols:] = dot(normed, w_ref[2]).astype(BF16)
    q_ref[...] = dot(normed, w_ref[0]).astype(BF16)


def qkv_of(grid, gain, weight, pad):
    cols = weight.shape[2]
    return call(
        qkv_kernel,
        [shape((pad, cols)), shape((pad, 2 * cols))],
        [grid, gain, weight],
        flops=2 * pad * weight.size,
        scratch=[pltpu.VMEM((pad, grid.shape[-1]), F32)],
    )


def attend_kernel(n_q, n_kv, resumed, final, pad, valid, *refs):
    q_refs, kv_refs, rest = refs[:n_q], refs[n_q : n_q + n_kv], refs[n_q + n_kv :]
    if resumed:
        (acc_in, top_in), rest = rest[:2], rest[2:]
    cols = q_refs[0].shape[1]
    low_lane = lax.broadcasted_iota(jnp.int32, (1, LANES), 1) < HD
    zero, one = jnp.zeros((), BF16), jnp.ones((), BF16)
    keys_count = sum(ref.shape[0] for ref in kv_refs)
    row = lax.broadcasted_iota(jnp.int32, (keys_count, 1), 0)
    real = lax.rem(row, pad) < valid
    tops = []
    for c in range(0, cols, LANES):
        q = jnp.concatenate([ref[:, c : c + LANES] for ref in q_refs], axis=0)
        keys = jnp.concatenate([ref[:, c : c + LANES] for ref in kv_refs], axis=0)
        values = jnp.concatenate(
            [ref[:, cols + c : cols + c + LANES] for ref in kv_refs], axis=0
        )
        parts = []
        for side in range(2):
            keep = low_lane if side == 0 else ~low_lane
            index = 2 * (c // LANES) + side
            scores = lax.dot_general(
                jnp.where(keep, q, zero), keys, (((1,), (1,)), ((), ())),
                preferred_element_type=F32,
            )
            top = jnp.max(scores, axis=-1, keepdims=True)
            if resumed:
                before = top_in[:, index : index + 1]
                top = jnp.maximum(top, before)
            probs = jnp.exp2((scores - top) * (HD ** (-0.5) * LOG2E)).astype(BF16)
            marked = jnp.where(real, jnp.where(keep, values, one), zero)
            mixed = dot(probs, marked)
            if resumed:
                lanes = slice(index * LANES, (index + 1) * LANES)
                decay = jnp.exp2((before - top) * (HD ** (-0.5) * LOG2E))
                mixed = mixed + acc_in[:, lanes] * decay
            if final:
                parts.append(mixed)
            else:
                rest[0][:, index * LANES : (index + 1) * LANES] = mixed
                tops.append(top)
        if final:
            mixed = jnp.where(low_lane, parts[0], parts[1])
            sums = pltpu.roll(jnp.where(low_lane, parts[1], parts[0]), HD, 1)
            out = (mixed / sums).astype(BF16)
            at = 0
            for o_ref in rest:
                o_ref[:, c : c + LANES] = out[at : at + o_ref.shape[0], :]
                at += o_ref.shape[0]
    if not final:
        for index, top in enumerate(tops):
            rest[1][:, index : index + 1] = top


def attend(queries, portions, pad, valid, state=None, pieces=None):
    cols = queries[0].shape[1]
    rows = sum(q.shape[0] for q in queries)
    keys = sum(p.shape[0] for p in portions)
    heads = cols // HD
    if pieces is None:
        outs = [shape((rows, heads * LANES), F32), shape((rows, LANES), F32)]
    else:
        outs = [shape((piece, cols)) for piece in pieces]
    return call(
        functools.partial(
            attend_kernel, len(queries), len(portions), state is not None, pieces is not None,
            pad, valid,
        ),
        outs,
        [*queries, *portions, *(state or ())],
        flops=8 * rows * keys * cols,
        exps=rows * keys * heads,
    )


def frame_out_kernel(n_head, n_piece, place_ref, *refs):
    x_refs, refs = refs[:n_head], refs[n_head:]
    att_ref, crossed_refs, refs = refs[0], refs[1:n_head], refs[n_head:]
    w_mine_ref, piece_refs = refs[0], refs[1 : 1 + (n_head - 1) * n_piece]
    gain_ref, w_ref = refs[1 + (n_head - 1) * n_piece : 3 + (n_head - 1) * n_piece]
    first_ref, q_own_ref, q_give_ref, kv_own_ref, kv_give_ref, rows_ref = refs[-6:]
    pad = first_ref.shape[0]
    place, parity = place_ref[0], place_ref[1]
    for d in range(n_head):
        gather_rows(rows_ref, d * pad, pad, x_refs[d])
    total = dot(att_ref[...], w_mine_ref[...])
    for e in range(1, n_head):
        for k in range(n_piece):
            piece_ref = piece_refs[(e - 1) * n_piece + k]
            share = piece_ref.shape[0]
            at = pl.multiple_of((place ^ k) * share, share)
            ref = crossed_refs[e - 1]
            part = jnp.concatenate(
                [
                    ref[(d ^ e) * pad : ((d ^ e) + 1) * pad, pl.ds(at, share)]
                    for d in range(n_head)
                ],
                axis=0,
            )
            total = total + dot(part, piece_ref[...])
    first = (rows_ref[...] + total).astype(BF16)
    first_ref[...] = first[:pad]
    normed = normalise(first.astype(F32), gain_ref[...], norm_eps).astype(BF16)
    half = q_own_ref.shape[1]
    own = pl.ds(pl.multiple_of(parity * half, half), half)
    give = pl.ds(pl.multiple_of((1 - parity) * half, half), half)
    for side, kv_ref in ((give, kv_give_ref), (own, kv_own_ref)):
        kv_ref[:, :half] = dot(normed, w_ref[1, :, side]).astype(BF16)
        kv_ref[:, half:] = dot(normed, w_ref[2, :, side]).astype(BF16)
    q_give_ref[...] = dot(normed, w_ref[0, :, give]).astype(BF16)
    q_own_ref[...] = dot(normed, w_ref[0, :, own]).astype(BF16)


def head_kernel(n_head, place_ref, first_ref, *refs):
    part_refs, refs = refs[: 2 * n_head], refs[2 * n_head :]
    w_refs, (gain_ref, proj_ref, bias_ref), refs = refs[:n_head], refs[n_head : n_head + 3], refs[n_head + 3 :]
    blocks_ref, projected_ref, top_ref, bottom_ref, rows_ref, edge_ref = refs
    width = first_ref.shape[1]
    half = part_refs[0].shape[1]
    parity = place_ref[1]
    first = first_ref[...].astype(F32)
    total = jnp.zeros(first.shape, F32)
    for a in range(2):
        for d in range(n_head):
            at = pl.multiple_of((parity ^ a) * half, half)
            total = total + dot(part_refs[a * n_head + d][...], w_refs[d][pl.ds(at, half), :])
    blocks = (first + total).astype(BF16).astype(F32)
    rows_ref[...] = blocks
    scatter_rows(blocks_ref, rows_ref)
    count = 2 * width
    mean = (
        jnp.sum(first, axis=-1, keepdims=True) + jnp.sum(blocks, axis=-1, keepdims=True)
    ) / count
    first, blocks = first - mean, blocks - mean
    spread = (
        jnp.sum(first * first, axis=-1, keepdims=True)
        + jnp.sum(blocks * blocks, axis=-1, keepdims=True)
    ) / count
    scale = lax.rsqrt(spread + head_eps)
    low = (first * scale * gain_ref[:, :width]).astype(BF16)
    high = (blocks * scale * gain_ref[:, width:]).astype(BF16)
    projected = dot(low, proj_ref[:width, :]) + dot(high, proj_ref[width:, :]) + bias_ref[...]
    projected_ref[...] = projected.astype(BF16)
    edge_ref[...] = projected
    _, height, columns, _ = blocks_ref.shape
    top_ref[...] = edge_ref[:columns, :].astype(BF16)
    bottom_ref[...] = edge_ref[(height - 1) * columns : height * columns, :].astype(BF16)


def conv_kernel(columns, count, projected_ref, w_ref, total_ref, rows_ref):
    pad = projected_ref.shape[0]
    margin = (rows_ref.shape[0] - pad) // 2
    rows_ref[...] = jnp.zeros(rows_ref.shape, F32)
    rows_ref[margin : margin + pad, :] = projected_ref[...].astype(F32)
    for extra in range(count, pad):
        rows_ref[margin + extra : margin + extra + 1, :] = jnp.zeros((1, rows_ref.shape[1]), F32)
    column = lax.rem(lax.broadcasted_iota(jnp.int32, (pad, 1), 0), columns)
    total = None
    for j in range(3):
        part = None
        for i in range(3):
            at = margin + (i - 1) * columns + j - 1
            term = dot(rows_ref[at : at + pad, :].astype(BF16), w_ref[i, j])
            part = term if part is None else part + term
        if j == 0:
            part = jnp.where(column > 0, part, 0.0)
        if j == 2:
            part = jnp.where(column < columns - 1, part, 0.0)
        total = part if total is None else total + part
    total_ref[...] = total


def edge_kernel(total_ref, low_ref, high_ref, w_ref, out_ref, rows_ref, sum_ref):
    _, height, columns, _ = out_ref.shape
    span = rows_ref.shape[0] - 16
    column = lax.broadcasted_iota(jnp.int32, (span, 1), 0)
    sum_ref[...] = total_ref[...]
    for i, ref, row in ((0, low_ref, 0), (2, high_ref, height - 1)):
        rows_ref[...] = jnp.zeros(rows_ref.shape, F32)
        rows_ref[8 : 8 + columns, :] = ref[...].astype(F32)
        total = None
        for j in range(3):
            part = dot(rows_ref[7 + j : 7 + j + span, :].astype(BF16), w_ref[i, j])
            if j == 0:
                part = jnp.where(column > 0, part, 0.0)
            if j == 2:
                part = jnp.where(column < columns - 1, part, 0.0)
            total = part if total is None else total + part
        at = slice(row * columns, (row + 1) * columns)
        sum_ref[at, :] = sum_ref[at, :] + total[:columns, :]
    scatter_rows(out_ref, sum_ref)


def on_device(
    tokens,
    frame_gain,
    frame_qkv,
    frame_out,
    global_gain,
    global_qkv,
    global_out,
    head_gain,
    head_proj,
    head_bias,
    head_conv,
):
    frames, height, width, depth = tokens.shape
    valid = frames * height * width
    pad = -(-valid // 16) * 16
    cols = frame_qkv.shape[2]
    half = cols // 2
    heads, seqs, bands = (lax.axis_size(name) for name in ("head", "seq", "band"))
    frame_gain, global_gain = frame_gain[None], global_gain[None]
    others = range(1, heads)

    by_pair = 2 if frame_out.shape[0] % (2 * bands * LANES) == 0 else 1
    parity, band = lax.axis_index("seq") % 2, lax.axis_index("band")
    place = (parity * bands if by_pair == 2 else 0) + band
    where = jnp.stack([place, parity]).astype(jnp.int32)
    share = frame_out.shape[0] // (bands * by_pair)
    part_out = lax.dynamic_slice_in_dim(frame_out, place * share, share, 0)

    grids = [tokens] + [swap(tokens, "head", d) for d in others]
    part_out, _ = lax.optimization_barrier((part_out, grids[-1]))
    pieces = []
    for d in others:
        mine = [swap(part_out, "head", d)]
        pair = [swap(mine[0], "seq", 1)] if by_pair == 2 else []
        crossed = [[swap(p, "band", b) for b in range(1, bands)] for p in mine + pair]
        for p, q in zip(mine + pair, crossed):
            pieces += [p, *q]
    projected = [qkv_of(grid, frame_gain, frame_qkv, pad) for grid in grids]
    keys = [kv for _, kv in projected]
    keys += [swap(kv, "band", b) for _, kv in projected for b in range(1, bands)]
    (attended,) = attend([q for q, _ in projected], keys, pad, valid, pieces=[heads * pad])
    crossed = [swap(attended, "head", d) for d in others]
    first, q_own, q_give, kv_own, kv_give = call(
        functools.partial(frame_out_kernel, heads, bands * by_pair),
        [
            shape((pad, depth)),
            shape((heads * pad, half)),
            shape((heads * pad, half)),
            shape((heads * pad, 2 * half)),
            shape((heads * pad, 2 * half)),
        ],
        [where, *grids, attended, *crossed, frame_out, *pieces, global_gain, global_qkv],
        flops=2 * heads * pad * depth * (heads * cols + 3 * cols),
        scratch=[pltpu.VMEM((heads * pad, depth), F32)],
    )

    late, _ = lax.optimization_barrier((global_out, crossed[-1]))
    out_weights = [global_out] + [swap(late, "head", d) for d in others]
    q_pair = swap(q_give, "seq", 1)
    chunks = [[kv_own], [swap(kv_give, "seq", 1)]]
    for distance in range(2, seqs):
        chunks.append([swap(kv_own if distance % 2 == 0 else kv_give, "seq", distance)])
    for chunk in chunks:
        chunk += [swap(chunk[0], "band", b) for b in range(1, bands)]
    chunks = [chunks[0] + chunks[1]] + chunks[2:]
    queries = [q_own, q_pair]
    if len(chunks) == 1:
        outs = attend(queries, chunks[0], pad, valid, pieces=[pad] * (2 * heads))
    else:
        state = None
        for chunk in chunks[:-1]:
            state = attend(queries, chunk, pad, valid, state)
        outs = attend(queries, chunks[-1], pad, valid, state, pieces=[pad] * (2 * heads))
    parts = []
    for a in range(2):
        for d in range(heads):
            piece = outs[a * heads + d]
            parts.append(piece if a + d == 0 else swap_both(piece, ("seq", "head"), (a, d)))

    channels = head_proj.shape[1]
    blocks, mapped, top, bottom = call(
        functools.partial(head_kernel, heads),
        [
            shape(tokens.shape),
            shape((pad, channels)),
            shape((width, channels)),
            shape((width, channels)),
        ],
        [where, first, *parts, *out_weights, head_gain[None], head_proj, head_bias[None]],
        flops=2 * pad * depth * (heads * cols + 2 * channels),
        scratch=[pltpu.VMEM((pad, depth), F32), pltpu.VMEM((pad, channels), F32)],
    )
    around = heads * bands
    low = lax.ppermute(bottom, ("head", "band"), [(i, i + 1) for i in range(around - 1)])
    high = lax.ppermute(top, ("head", "band"), [(i + 1, i) for i in range(around - 1)])
    margin = -(-(width + 1) // 8) * 8
    (total,) = call(
        functools.partial(conv_kernel, width, valid),
        [shape((pad, channels), F32)],
        [mapped, head_conv],
        flops=2 * pad * head_conv.size,
        scratch=[pltpu.VMEM((pad + 2 * margin, channels), F32)],
    )
    span = -(-width // 8) * 8
    (features,) = call(
        edge_kernel,
        [shape((*tokens.shape[:3], channels))],
        [total, low, high, head_conv],
        flops=4 * span * channels * channels * 3,
        scratch=[pltpu.VMEM((span + 16, channels), F32), pltpu.VMEM((pad, channels), F32)],
    )
    return (blocks, features)


def solution(mesh):
    rows = P(("scene", "seq"), ("head", "band"), None, None)
    columns, out_rows = P(None, None, "head"), P("head", None)
    return jax.shard_map(
        on_device,
        mesh=mesh,
        in_specs=(rows, P(), columns, out_rows, P(), columns, out_rows, P(), P(), P(), P()),
        out_specs=(rows, rows),
        check_vma=False,
    )
```

```python
import functools

import jax
import jax.numpy as jnp
from jax import lax
from jax.experimental import pallas as pl
from jax.experimental.pallas import tpu as pltpu
from jax.sharding import PartitionSpec as P


HD = 64
LANES = 128
LOG2E = 1.4426950408889634
UNIT = HD ** (-0.5) * LOG2E

norm_eps = 1e-06
head_eps = 1e-05

VM = pl.BlockSpec(memory_space=pltpu.VMEM)
SM = pl.BlockSpec(memory_space=pltpu.SMEM)
F32 = jnp.float32
BF16 = jnp.bfloat16


def swap(value, axis, distance):
    size = lax.axis_size(axis)
    return lax.ppermute(value, axis, [(i, i ^ distance) for i in range(size)])


def swap_both(value, axes, distances):
    (outer, inner), (a, b) = axes, distances
    if a == 0 or b == 0:
        return swap(value, inner if a == 0 else outer, a + b)
    rows, cols = lax.axis_size(outer), lax.axis_size(inner)
    pairs = [
        (i * cols + j, (i ^ a) * cols + (j ^ b)) for i in range(rows) for j in range(cols)
    ]
    return lax.ppermute(value, axes, pairs)


def call(kernel, outs, args, flops=0, exps=0, scratch=(), limit=16 << 20, whole=()):
    moved = sum(a.size * a.dtype.itemsize for a in args)
    moved += sum(o.size * o.dtype.itemsize for o in outs)
    specs = [SM if a.dtype == jnp.int32 else VM for a in args]
    return pl.pallas_call(
        kernel,
        out_shape=[pltpu.VMEM(o.shape, o.dtype) for o in outs],
        in_specs=specs + [pl.BlockSpec(memory_space=pl.ANY)] * len(whole),
        out_specs=[VM] * len(outs),
        scratch_shapes=list(scratch),
        compiler_params=pltpu.CompilerParams(vmem_limit_bytes=limit),
        cost_estimate=pl.CostEstimate(
            flops=int(flops), transcendentals=int(exps), bytes_accessed=int(moved)
        ),
    )(*args, *whole)


def shape(dims, dtype=BF16):
    return jax.ShapeDtypeStruct(tuple(dims), dtype)


def dot(a, b):
    return jnp.dot(a, b, preferred_element_type=F32)


def normalise(values, gain, epsilon):
    centre = values - jnp.mean(values, axis=-1, keepdims=True)
    spread = jnp.mean(centre * centre, axis=-1, keepdims=True)
    return centre * lax.rsqrt(spread + epsilon) * gain


def gather_rows(rows_ref, base, pad, grid_ref):
    frames, height, width, _ = grid_ref.shape
    at = base
    for f in range(frames):
        for r in range(height):
            rows_ref[at : at + width, :] = grid_ref[f, r].astype(F32)
            at += width
    last = grid_ref[frames - 1, height - 1, width - 1 : width, :].astype(F32)
    for extra in range(at, base + pad):
        rows_ref[extra : extra + 1, :] = last


def scatter_rows(grid_ref, rows_ref):
    frames, height, width, _ = grid_ref.shape
    at = 0
    for f in range(frames):
        for r in range(height):
            grid_ref[f, r] = rows_ref[at : at + width, :].astype(grid_ref.dtype)
            at += width


def qkv_kernel(x_ref, gain_ref, w_ref, q_ref, kv_ref, rows_ref):
    cols = q_ref.shape[1]
    gather_rows(rows_ref, 0, rows_ref.shape[0], x_ref)
    normed = normalise(rows_ref[...], gain_ref[...], norm_eps).astype(BF16)
    kv_ref[:, :cols] = dot(normed, w_ref[1]).astype(BF16)
    kv_ref[:, cols:] = dot(normed, w_ref[2]).astype(BF16)
    q_ref[...] = (dot(normed, w_ref[0]) * UNIT).astype(BF16)


def qkv_of(grid, gain, weight, pad):
    cols = weight.shape[2]
    return call(
        qkv_kernel,
        [shape((pad, cols)), shape((pad, 2 * cols))],
        [grid, gain, weight],
        flops=2 * pad * weight.size,
        scratch=[pltpu.VMEM((pad, grid.shape[-1]), F32)],
    )


def softmax_pass(queries, keys, values, before=None):
    rows = queries.shape[0]
    both = jnp.concatenate([own_lanes(queries, 0), own_lanes(queries, 1)], axis=0)
    scores = lax.dot_general(both, keys, (((1,), (1,)), ((), ())), preferred_element_type=F32)
    top = jnp.max(scores, axis=-1, keepdims=True)
    if before is not None:
        top = jnp.maximum(top, before)
    mixed = dot(jnp.exp2(scores - top).astype(BF16), values)
    low, high = mixed[:rows], mixed[rows:]
    keep = lanes_of(0)
    weighted = jnp.where(keep, low[:, :LANES], high[:, :LANES])
    sums = jnp.where(keep, low[:, LANES:], high[:, LANES:])
    return weighted, sums, top


def lanes_of(side):
    lane = lax.broadcasted_iota(jnp.int32, (1, LANES), 1)
    return lane < HD if side == 0 else lane >= HD


def joined(refs, at, width):
    return jnp.concatenate([ref[:, at : at + width] for ref in refs], axis=0)


def real_rows(count, pad, valid):
    return lax.rem(lax.broadcasted_iota(jnp.int32, (count, 1), 0), pad) < valid


def marked(values, real):
    zero, one = jnp.zeros((), BF16), jnp.ones((), BF16)
    ones = jnp.broadcast_to(jnp.where(real, one, zero), values.shape)
    return jnp.concatenate([jnp.where(real, values, zero), ones], axis=1)


def own_lanes(tile, side):
    return jnp.where(lanes_of(side), tile, jnp.zeros((), BF16))


def frame_kernel(n_kv, pad, valid, q_ref, *refs):
    kv_refs, (w_ref, o_ref, mixed_ref) = refs[:n_kv], refs[n_kv:]
    cols = q_ref.shape[1]
    real = real_rows(sum(ref.shape[0] for ref in kv_refs), pad, valid)
    for c in range(0, cols, LANES):
        q = q_ref[:, c : c + LANES]
        keys, values = joined(kv_refs, c, LANES), joined(kv_refs, cols + c, LANES)
        weighted, sums, _ = softmax_pass(q, keys, marked(values, real))
        mixed_ref[:, c : c + LANES] = (weighted / sums).astype(BF16)
    o_ref[...] = dot(mixed_ref[...], w_ref[...]).astype(BF16)


def frame_attend(q, portions, weight, pad, valid):
    keys = sum(p.shape[0] for p in portions)
    rows, cols = q.shape
    return call(
        functools.partial(frame_kernel, len(portions), pad, valid),
        [shape((rows, weight.shape[1]))],
        [q, *portions, weight],
        flops=rows * cols * (8 * keys + 2 * weight.shape[1]),
        exps=rows * keys * cols // HD,
        scratch=[pltpu.VMEM((rows, cols), BF16)],
    )[0]


def scene_kernel(cols, n_q, n_kv, offsets, resumed, final, pad, valid, *refs):
    q_refs, kv_refs, refs = refs[:n_q], refs[n_q : n_q + n_kv], refs[n_q + n_kv :]
    states, outs = (refs[:2], refs[2:]) if resumed else ((), refs)
    rows = sum(ref.shape[0] for ref in q_refs)
    real = real_rows(sum(ref.shape[0] for ref in kv_refs), pad, valid)
    for c in range(0, cols, LANES):
        q = joined(q_refs, c, LANES)
        keys = jnp.concatenate(
            [ref[:, o + c : o + c + LANES] for ref, o in zip(kv_refs, offsets)], axis=0
        )
        values = jnp.concatenate(
            [ref[:, o + cols + c : o + cols + c + LANES] for ref, o in zip(kv_refs, offsets)],
            axis=0,
        )
        tile = c // LANES
        before = states[1][:, tile : tile + 1] if resumed else None
        weighted, sums, top = softmax_pass(q, keys, marked(values, real), before)
        if resumed:
            decay = jnp.exp2(before - top)
            decay = jnp.where(lanes_of(0), decay[:rows], decay[rows:])
            weighted = weighted + states[0][:, 2 * c : 2 * c + LANES] * decay
            sums = sums + states[0][:, 2 * c + LANES : 2 * c + 2 * LANES] * decay
        if final:
            out, at = (weighted / sums).astype(BF16), 0
            for ref in outs:
                ref[:, c : c + LANES] = out[at : at + ref.shape[0]]
                at += ref.shape[0]
        else:
            outs[0][:, 2 * c : 2 * c + LANES] = weighted
            outs[0][:, 2 * c + LANES : 2 * c + 2 * LANES] = sums
            outs[1][:, tile : tile + 1] = top


def scene_attend(queries, cols, portions, pad, valid, states=None, pieces=None):
    rows = sum(q.shape[0] for q in queries)
    keys = sum(p.shape[0] for p, _ in portions)
    if pieces is None:
        outs = [shape((rows, 2 * cols), F32), shape((2 * rows, LANES), F32)]
    else:
        outs = [shape((piece, cols)) for piece in pieces]
    return call(
        functools.partial(
            scene_kernel, cols, len(queries), len(portions), [o for _, o in portions],
            states is not None, pieces is not None, pad, valid,
        ),
        outs,
        [*queries, *(p for p, _ in portions), *(states or ())],
        flops=8 * rows * keys * cols,
        exps=rows * keys * cols // HD,
    )


def second_qkv_kernel(n_part, sharing, keeping, x_ref, *refs):
    part_refs, refs = refs[:n_part], refs[n_part:]
    gain_ref, w_ref, refs = refs[0], refs[1], refs[2:]
    if sharing:
        whole_ref, share_ref, sem = refs[0], refs[1], refs[-1]
        rows = share_ref.shape[0]
        at = pl.multiple_of(lax.axis_index("band") * rows, rows)
        copy = pltpu.make_async_copy(whole_ref.at[pl.ds(at, rows), :], share_ref, sem)
        copy.start()
        refs = refs[2:-1]
    if keeping:
        first_ref, refs = refs[0], refs[1:]
    q_own_ref, kv_own_ref, give_ref, kv_give_ref, rows_ref = refs
    pad = rows_ref.shape[0]
    parity = lax.rem(lax.axis_index("seq"), 2)
    gather_rows(rows_ref, 0, pad, x_ref)
    total = part_refs[0][...].astype(F32)
    for ref in part_refs[1:]:
        total = total + ref[...].astype(F32)
    first = (rows_ref[...] + total).astype(BF16)
    if keeping:
        first_ref[...] = first
    normed = normalise(first.astype(F32), gain_ref[...], norm_eps).astype(BF16)
    half = q_own_ref.shape[1]
    own = pl.ds(pl.multiple_of(parity * half, half), half)
    give = pl.ds(pl.multiple_of((1 - parity) * half, half), half)
    for t in (1, 2):
        kv_own_ref[:, (t - 1) * half : t * half] = dot(normed, w_ref[t, :, own]).astype(BF16)
        part = dot(normed, w_ref[t, :, give]).astype(BF16)
        kv_give_ref[:, (t - 1) * half : t * half] = part
        give_ref[:, t * half : (t + 1) * half] = part
    give_ref[:, :half] = (dot(normed, w_ref[0, :, give]) * UNIT).astype(BF16)
    q_own_ref[...] = (dot(normed, w_ref[0, :, own]) * UNIT).astype(BF16)
    if sharing:
        copy.wait()


def second_qkv(grid, parts, gain, weight, pad, keeping, shared=None, bands=1):
    depth, half = grid.shape[-1], weight.shape[2] // 2
    outs = [shape((pad, width)) for width in (half, 2 * half, 3 * half, 2 * half)]
    scratch = [pltpu.VMEM((pad, depth), F32)]
    if keeping:
        outs = [shape((pad, depth))] + outs
    if shared is not None:
        outs = [shape((shared.shape[0] // bands, shared.shape[1]))] + outs
        scratch.append(pltpu.SemaphoreType.DMA)
    return call(
        functools.partial(second_qkv_kernel, len(parts), shared is not None, keeping),
        outs,
        [grid, *parts, gain, weight],
        flops=2 * pad * weight.size,
        scratch=scratch,
        whole=[] if shared is None else [shared],
    )


def head_kernel(n_head, n_part, first_ref, *refs):
    piece_refs, refs = refs[: 2 * n_head], refs[2 * n_head :]
    w_ref, share_refs, refs = refs[0], refs[1 : 1 + (n_head - 1) * n_part], refs[1 + (n_head - 1) * n_part :]
    gain_ref, proj_ref, bias_ref = refs[:3]
    blocks_ref, projected_ref, near_ref, far_ref, rows_ref, edge_ref = refs[3:]
    width = first_ref.shape[1]
    half = piece_refs[0].shape[1]
    parity, band = lax.rem(lax.axis_index("seq"), 2), lax.axis_index("band")
    first = first_ref[...].astype(F32)
    total = jnp.zeros(first.shape, F32)
    for a in range(2):
        at = (parity ^ a) * half
        mine = w_ref[pl.ds(pl.multiple_of(at, half), half), :]
        total = total + dot(piece_refs[a * n_head][...], mine)
    for d in range(1, n_head):
        pair = [piece_refs[a * n_head + d][...] for a in range(2)]
        even = parity == 0
        row = jnp.concatenate(
            [jnp.where(even, pair[0], pair[1]), jnp.where(even, pair[1], pair[0])], axis=1
        )
        rows = row.shape[1] // n_part
        for k in range(n_part):
            part = row[:, :rows]
            for other in range(1, n_part):
                part = jnp.where((band ^ k) == other, row[:, other * rows : (other + 1) * rows], part)
            total = total + dot(part, share_refs[(d - 1) * n_part + k][...])
    blocks = (first + total).astype(BF16).astype(F32)
    rows_ref[...] = blocks
    scatter_rows(blocks_ref, rows_ref)
    count = 2 * width
    mean = (
        jnp.sum(first, axis=-1, keepdims=True) + jnp.sum(blocks, axis=-1, keepdims=True)
    ) / count
    first, blocks = first - mean, blocks - mean
    spread = (
        jnp.sum(first * first, axis=-1, keepdims=True)
        + jnp.sum(blocks * blocks, axis=-1, keepdims=True)
    ) / count
    scale = lax.rsqrt(spread + head_eps)
    low = (first * scale * gain_ref[:, :width]).astype(BF16)
    high = (blocks * scale * gain_ref[:, width:]).astype(BF16)
    projected = dot(low, proj_ref[:width, :]) + dot(high, proj_ref[width:, :]) + bias_ref[...]
    projected_ref[...] = projected.astype(BF16)
    edge_ref[...] = projected
    _, height, columns, _ = blocks_ref.shape
    top = edge_ref[:columns, :]
    bottom = edge_ref[(height - 1) * columns : height * columns, :]
    even = lax.rem(band, 2) == 0
    near_ref[...] = jnp.where(even, bottom, top).astype(BF16)
    far_ref[...] = jnp.where(even, top, bottom).astype(BF16)


def conv_kernel(columns, count, projected_ref, w_ref, total_ref, rows_ref):
    pad = projected_ref.shape[0]
    margin = (rows_ref.shape[0] - pad) // 2
    rows_ref[...] = jnp.zeros(rows_ref.shape, F32)
    rows_ref[margin : margin + pad, :] = projected_ref[...].astype(F32)
    for extra in range(count, pad):
        rows_ref[margin + extra : margin + extra + 1, :] = jnp.zeros((1, rows_ref.shape[1]), F32)
    column = lax.rem(lax.broadcasted_iota(jnp.int32, (pad, 1), 0), columns)
    total = None
    for j in range(3):
        part = None
        for i in range(3):
            at = margin + (i - 1) * columns + j - 1
            term = dot(rows_ref[at : at + pad, :].astype(BF16), w_ref[i, j])
            part = term if part is None else part + term
        if j == 0:
            part = jnp.where(column > 0, part, 0.0)
        if j == 2:
            part = jnp.where(column < columns - 1, part, 0.0)
        total = part if total is None else total + part
    total_ref[...] = total


def edge_kernel(total_ref, near_ref, far_ref, w_ref, out_ref, rows_ref, sum_ref):
    _, height, columns, _ = out_ref.shape
    span = rows_ref.shape[0] - 16
    column = lax.broadcasted_iota(jnp.int32, (span, 1), 0)
    sum_ref[...] = total_ref[...]
    even = lax.rem(lax.axis_index("band"), 2) == 0
    near, far = near_ref[...].astype(F32), far_ref[...].astype(F32)
    low, high = jnp.where(even, far, near), jnp.where(even, near, far)
    for i, edge, row in ((0, low, 0), (2, high, height - 1)):
        rows_ref[...] = jnp.zeros(rows_ref.shape, F32)
        rows_ref[8 : 8 + columns, :] = edge
        total = None
        for j in range(3):
            part = dot(rows_ref[7 + j : 7 + j + span, :].astype(BF16), w_ref[i, j])
            if j == 0:
                part = jnp.where(column > 0, part, 0.0)
            if j == 2:
                part = jnp.where(column < columns - 1, part, 0.0)
            total = part if total is None else total + part
        at = slice(row * columns, (row + 1) * columns)
        sum_ref[at, :] = sum_ref[at, :] + total[:columns, :]
    scatter_rows(out_ref, sum_ref)


def on_device(
    tokens,
    frame_gain,
    frame_qkv,
    frame_out,
    global_gain,
    global_qkv,
    global_out,
    head_gain,
    head_proj,
    head_bias,
    head_conv,
):
    frames, height, width, depth = tokens.shape
    valid = frames * height * width
    pad = -(-valid // 16) * 16
    cols = frame_qkv.shape[2]
    half = cols // 2
    heads, seqs, bands = (lax.axis_size(name) for name in ("head", "seq", "band"))
    frame_gain, global_gain = frame_gain[None], global_gain[None]
    others = range(1, heads)

    def over_band(value):
        return [swap(value, "band", b) for b in range(1, bands)]

    grids = [tokens] + [swap(tokens, "head", d) for d in others]
    qkv = [qkv_of(grids[d], frame_gain, frame_qkv, pad) for d in range(heads)]
    keys = [kv for _, kv in qkv]
    keys += [p for _, kv in qkv for p in over_band(kv)]
    sums = [[None] * heads for _ in range(heads)]
    for d in reversed(range(heads)):
        part = frame_attend(qkv[d][0], keys, frame_out, pad, valid)
        sums[d][0] = part
        for e in others:
            sums[d ^ e][e] = swap(part, "head", e)
    seconds = []
    for d in range(heads):
        shared = global_out if d == heads - 1 else None
        seconds.append(
            second_qkv(grids[d], sums[d], global_gain, global_qkv, pad, d == 0, shared, bands)
        )
    shares = []
    for d in others:
        mine = swap(seconds[-1][0], "head", d)
        shares += [mine] + over_band(mine)

    own, pair, far = [], [], [[] for _ in range(2, seqs)]
    q_own, q_pair = [], []
    for *_, q, kv, give, kv_give in seconds:
        q_own.append(q)
        own.append([(p, 0) for p in [kv] + over_band(kv)])
        given = swap(give, "seq", 1)
        q_pair.append(given)
        pair.append([(p, half) for p in [given] + over_band(given)])
        for k in range(2, seqs):
            moved = swap(kv if k % 2 == 0 else kv_give, "seq", k)
            far[k - 2].append([(p, 0) for p in [moved] + over_band(moved)])

    def passes(queries, early, late):
        most = max(28 // heads, 1)
        chunks = []
        for portions in (sum(early, []), sum(late, [])):
            for begin in range(0, len(portions), most):
                chunks.append(portions[begin : begin + most])
        states = None
        for chunk in chunks[:-1]:
            states = scene_attend(queries, half, chunk, pad, valid, states)
        late = chunks[-1]
        return scene_attend(queries, half, late, pad, valid, states, [pad] * heads)

    outs_own = passes(
        q_own, own + pair[:1] + [f[0] for f in far], pair[1:] + [p for f in far for p in f[1:]]
    )
    outs_pair = passes(
        q_pair,
        own + pair + [p for f in far[:-1] for p in f] + [f[0] for f in far[-1:]],
        [p for f in far[-1:] for p in f[1:]],
    )
    pieces = []
    for a, outs in enumerate((outs_own, outs_pair)):
        for d, piece in enumerate(outs):
            if a + d > 0:
                piece = swap_both(piece, ("seq", "head"), (a, d))
            pieces.append(piece)

    channels = head_proj.shape[1]
    blocks, mapped, near, away = call(
        functools.partial(head_kernel, heads, bands),
        [
            shape(tokens.shape),
            shape((pad, channels)),
            shape((width, channels)),
            shape((width, channels)),
        ],
        [seconds[0][0], *pieces, global_out, *shares, head_gain[None], head_proj,
         head_bias[None]],
        flops=2 * pad * depth * (heads * cols + 2 * channels),
        scratch=[pltpu.VMEM((pad, depth), F32), pltpu.VMEM((pad, channels), F32)],
    )
    around = heads * bands
    links = [(i, i ^ 1) for i in range(around)]
    near = lax.ppermute(near, ("head", "band"), links)
    links = [(i, i + 1) for i in range(1, around - 1, 2)]
    away = lax.ppermute(away, ("head", "band"), links + [(j, i) for i, j in links])
    margin = -(-(width + 1) // 8) * 8
    (total,) = call(
        functools.partial(conv_kernel, width, valid),
        [shape((pad, channels), F32)],
        [mapped, head_conv],
        flops=2 * pad * head_conv.size,
        scratch=[pltpu.VMEM((pad + 2 * margin, channels), F32)],
    )
    span = -(-width // 8) * 8
    (features,) = call(
        edge_kernel,
        [shape((*tokens.shape[:3], channels))],
        [total, near, away, head_conv],
        flops=4 * span * channels * channels * 3,
        scratch=[pltpu.VMEM((span + 16, channels), F32), pltpu.VMEM((pad, channels), F32)],
    )
    return (blocks, features)


def solution(mesh):
    rows = P(("scene", "seq"), ("head", "band"), None, None)
    columns, out_rows = P(None, None, "head"), P("head", None)

    return jax.shard_map(
        on_device,
        mesh=mesh,
        in_specs=(rows, P(), columns, out_rows, P(), columns, out_rows, P(), P(), P(), P()),
        out_specs=(rows, rows),
        check_vma=False,
    )
```
